32 devices in a mesh: tm: 4 (over y, core), height: 8 (over z, x).
Axes of the slice: x: 2, y: 2, z: 4, core: 2. Of those that a mesh axis runs over, the one named last changes fastest.
Arguments:
- latents: bfloat16 [2, 16, 32, 16, 384], P(None, 'tm', 'height'), may hold values from -6 to 6
- conv_in: bfloat16 [3, 3, 3, 384, 192], replicated, may hold values from -0.0625 to 0.0625
- conv_out: bfloat16 [3, 3, 3, 192, 192], replicated, may hold values from -0.078125 to 0.078125
- shortcut: bfloat16 [384, 192], replicated, may hold values from -0.3125 to 0.3125
- norm_gain: float32 [192], replicated, may hold values from 0.1 to 1.9
- video_rows: int32 [2], replicated, may hold values from 8 to 32, as said below
- video_cols: int32 [2], replicated, may hold values from 4 to 16, as said below
Outputs:
- decoded: bfloat16 [2, 16, 64, 32, 192], P(None, 'tm', 'height')
The draws below stay inside these ranges and needn't reach their ends.
Inputs may be any that keep to these rules, and one draw needn't show every extreme that they name: `video_rows`: some video uses all 32 rows in every draw. `video_cols`: some video uses all 16 columns in every draw.
All inputs are finite; a program needn't handle non-finite values.
Results may differ from the reference program's by a relative error of at most 0.0032.
Values may be sent and summed in bfloat16 or wider, within the bound.
A program may use at most 128 MiB of HBM per device.

```python
import jax
import jax.numpy as jnp
from jax import lax

C_IN = 384
C_OUT = 192
VIDEOS = 2
COLS = 16
FRAMES = 16
ROWS = 32


def forced_most(key, salt, most):
    first, second = jax.random.split(jax.random.fold_in(key, salt))
    values = jax.random.randint(first, (VIDEOS,), most // 4, most + 1)
    picked = jax.random.randint(second, (), 0, VIDEOS)
    return jnp.where(jnp.arange(VIDEOS) == picked, most, values).astype(jnp.int32)


def draw_video_rows(key, part):
    return forced_most(key, 11, ROWS)


def draw_video_cols(key, part):
    return forced_most(key, 23, COLS)


def shard_levels(own_key, shape, shards, least, high):
    loudness, own = 1.0, jax.random.fold_in(own_key, 6)
    for dim, parts in shards:
        steps = jnp.exp(jax.random.uniform(jax.random.fold_in(own, dim), (parts,), jnp.float32, least / len(shards), high / len(shards)))
        loudness = loudness * jnp.repeat(steps, shape[dim] // parts).reshape([-1 if axis == dim else 1 for axis in range(len(shape))])
    return loudness


def scatter_about(own_key, shape, deviation, most, cuts=(), held_as=jnp.bfloat16):
    entries = deviation * jax.random.normal(own_key, shape, jnp.float32)
    if cuts:
        entries = entries * shard_levels(own_key, shape, cuts, -0.22, 0.18)
    return jnp.clip(entries, -most, most).astype(held_as)


def setup_inputs(seed: int = 0) -> dict:
    seeds = jax.random.split(jax.random.key(seed), 8)
    return {
        "latents": scatter_about(seeds[0], (VIDEOS, FRAMES, ROWS, COLS, C_IN), 1.0, 6.0, ((1, 4), (2, 8))),
        "conv_in": scatter_about(seeds[1], (3, 3, 3, C_IN, C_OUT), (27 * C_IN) ** -0.5, 0.0625),
        "conv_out": scatter_about(seeds[2], (3, 3, 3, C_OUT, C_OUT), (27 * C_OUT) ** -0.5, 0.078125),
        "shortcut": scatter_about(seeds[3], (C_IN, C_OUT), C_IN ** -0.5, 0.3125),
        "norm_gain": jnp.clip(1.0 + 0.18 * jax.random.normal(seeds[4], (C_OUT,), jnp.float32), 0.1, 1.9),
        "video_rows": draw_video_rows(jax.random.fold_in(seeds[7], 71), 0),
        "video_cols": draw_video_cols(jax.random.fold_in(seeds[7], 71), 0),
    }


def causal_conv(padded, weight):
    videos, frames_in, rows_in, cols_in, chans = padded.shape
    frames_out = frames_in - 2
    rows_out = rows_in - 2
    cols_out = cols_in - 2
    outputs = weight.shape[-1]
    total = jnp.zeros((videos * frames_out * rows_out * cols_out, outputs), jnp.float32)
    for frame_tap in range(3):
        for row_tap in range(3):
            window = padded[:, frame_tap:frame_tap + frames_out, row_tap:row_tap + rows_out]
            stacked = jnp.concatenate([window[:, :, :, col_tap:col_tap + cols_out] for col_tap in range(3)], axis=-1)
            total = total + jnp.dot(stacked.reshape(-1, 3 * chans), weight[frame_tap, row_tap].reshape(3 * chans, outputs), preferred_element_type=jnp.float32)
    return total.reshape(videos, frames_out, rows_out, cols_out, outputs)

def reference(latents, conv_in, conv_out, shortcut, norm_gain, video_rows, video_cols):

    def one_video(packed):
        frames_all, used_rows, used_cols = packed
        row_ids = jnp.arange(ROWS, dtype=jnp.int32)
        col_ids = jnp.arange(COLS, dtype=jnp.int32)
        keep_in = (row_ids[:, None] < used_rows) & (col_ids[None, :] < used_cols)
        masked = jnp.where(keep_in[None, :, :, None], frames_all, jnp.zeros_like(frames_all))
        upsampled = jnp.repeat(jnp.repeat(masked, 2, axis=1), 2, axis=2)
        padded = jnp.pad(upsampled, ((2, 0), (1, 1), (1, 1), (0, 0)))
        hidden = causal_conv(padded[None], conv_in)[0]
        scale = lax.rsqrt(lax.optimization_barrier(jnp.mean(hidden * hidden, axis=-1, keepdims=True)) + 1e-06)
        normed = hidden * scale * norm_gain
        out_rows = jnp.arange(2 * ROWS, dtype=jnp.int32)
        out_cols = jnp.arange(2 * COLS, dtype=jnp.int32)
        keep_out = (out_rows[:, None] < 2 * used_rows) & (out_cols[None, :] < 2 * used_cols)
        gated = jnp.where(keep_out[None, :, :, None], jax.nn.silu(normed), jnp.zeros_like(normed)).astype(jnp.bfloat16)
        gated_pad = jnp.pad(gated, ((2, 0), (1, 1), (1, 1), (0, 0)))
        result = causal_conv(gated_pad[None], conv_out)[0]
        short = jnp.dot(upsampled.reshape(-1, C_IN), shortcut, preferred_element_type=jnp.float32).reshape(result.shape)
        summed = result + short
        return jnp.where(keep_out[None, :, :, None], summed, jnp.zeros_like(summed)).astype(jnp.bfloat16)
    return lax.map(one_video, (latents, video_rows, video_cols))
```

```python
import functools

import jax
import jax.numpy as jnp
from jax import lax
from jax.experimental import pallas as pl
from jax.experimental.pallas import tpu as pltpu
from jax.sharding import PartitionSpec as P

BF = jnp.bfloat16
F32 = jnp.float32


def section(
    total_rows,
    rows_ref,
    cols_ref,
    pos_ref,
    own_ref,
    prev_ref,
    top_ref,
    bot_ref,
    ptop_ref,
    pbot_ref,
    w1_ref,
    w2_ref,
    ws_ref,
    gain_ref,
    out_ref,
    xm,
    prod,
    gat,
    padded_gain,
):
    videos, frames, rows, cols, chans = own_ref.shape
    outs = out_ref.shape[-1]
    ext = rows + 2
    held = frames + 2
    band = pos_ref[0] * rows
    col_in = lax.broadcasted_iota(jnp.int32, (cols, 1), 0)

    for v in range(videos):
        limit_row, limit_col = rows_ref[v], cols_ref[v]
        keep_col = col_in < limit_col
        for r in range(ext):
            row = band + r - 1
            keep = keep_col & ((row >= 0) & (row < limit_row))
            for src, psrc, at in (
                ((top_ref, ptop_ref, 0),) if r == 0 else ((bot_ref, pbot_ref, 0),) if r == ext - 1 else ((own_ref, prev_ref, r - 1),)
            ):
                for t in range(frames):
                    old = psrc[v, t, at]
                    new = src[v, t, at]
                    xm[v, t, r] = jnp.where(keep, old, jnp.zeros_like(old))
                    xm[v, frames + t, r] = jnp.where(keep, new, jnp.zeros_like(new))

    low = ext * cols
    half = 2 * rows * cols
    first = col_in == 0
    last = col_in == cols - 1
    wide = gat.shape[-1]
    padded_gain[...] = jnp.zeros_like(padded_gain)
    padded_gain[:, :outs] = gain_ref[...]
    gain = padded_gain[...]
    place = lax.broadcasted_iota(jnp.int32, (2 * half, 2 * half), 0)
    taken = lax.broadcasted_iota(jnp.int32, (2 * half, 2 * half), 1)
    inner = place % (2 * cols)
    wanted = (inner % 2) * half + (place // (2 * cols)) * cols + inner // 2
    perm = (taken == wanted).astype(BF)
    spot = lax.broadcasted_iota(jnp.int32, (2 * half, 1), 0)
    spot_row = band * 2 + spot // (2 * cols)
    spot_col = spot % (2 * cols)
    low_zeros = jnp.zeros((wide - outs, 3 * chans), BF)
    mid_zeros = jnp.zeros((wide - outs, outs), BF)
    planes_of = ((0, 1, 2), (1, 2, 3))

    def products(v):
        lhs = jnp.concatenate(
            [xm[v, frames - 4 + a : frames - 4 + a + held].reshape(held * low, chans) for a in range(3)],
            axis=-1,
        )
        for b in range(3):
            for c in range(3):
                weight = jnp.concatenate([w1_ref[a, b, c] for a in range(3)], axis=-1)
                weight = jnp.concatenate([weight, low_zeros], axis=0)
                prod[v, b, c] = lax.dot_general(
                    lhs, weight, (((1,), (1,)), ((), ())), preferred_element_type=F32
                ).reshape(held, ext, cols, wide)

    def gate(v, f):
        keep_col = col_in < cols_ref[v]
        for i in range(2 * rows + 2):
            l = (i + 1) // 2
            pick = (l, l, l + 1) if i % 2 == 0 else (l - 1, l, l)
            summed = [
                prod[v, 0, c, f, pick[0]] + prod[v, 1, c, f, pick[1]] + prod[v, 2, c, f, pick[2]]
                for c in range(3)
            ]
            row = band * 2 + i - 1
            keep = keep_col & ((row >= 0) & (row < 2 * rows_ref[v]))
            left = jnp.where(first, 0.0, pltpu.roll(summed[0], 1, 0))
            right = jnp.where(last, 0.0, pltpu.roll(summed[2], cols - 1, 0))
            planes = []
            for hidden in (left + summed[1] + summed[2], summed[0] + summed[1] + right):
                mean = jnp.sum(hidden * hidden, axis=-1, keepdims=True) * (1.0 / outs)
                normed = hidden * lax.rsqrt(mean + 1e-06) * gain
                act = 0.5 * normed * (1.0 + jnp.tanh(0.5 * normed))
                planes.append(jnp.where(keep, act, 0.0) if True else act)
            even, odd = planes
            before = jnp.where(first, 0.0, pltpu.roll(odd, 1, 0))
            after = jnp.where(last, 0.0, pltpu.roll(even, cols - 1, 0))
            for at, plane in enumerate((before, even, odd, after)):
                gat[v, at, f, i] = plane.astype(BF)

    def finish(v, t):
        short = lax.dot_general(
            xm[v, frames + t, 1 : 1 + rows].reshape(rows * cols, chans),
            ws_ref[...],
            (((1,), (1,)), ((), ())),
            preferred_element_type=F32,
        ).reshape(rows, 1, cols, outs)
        short = jnp.broadcast_to(short, (rows, 2, cols, outs)).reshape(half, outs)
        lhs = jnp.concatenate(
            [
                jnp.concatenate(
                    [
                        gat[v, planes_of[p][c], t + a, b : b + 2 * rows].reshape(half, wide)
                        for p in range(2)
                    ],
                    axis=0,
                )
                for a in range(3)
                for b in range(3)
                for c in range(3)
            ],
            axis=-1,
        )
        weight = jnp.concatenate(
            [
                piece
                for a in range(3)
                for b in range(3)
                for c in range(3)
                for piece in (w2_ref[a, b, c], mid_zeros)
            ],
            axis=0,
        )
        total = jnp.zeros((2 * half, outs), F32)
        for k in range(27):
            total = total + jnp.dot(lhs[:, k * wide : k * wide + outs], weight[k * wide : k * wide + outs], preferred_element_type=F32)
        total = total + jnp.concatenate([short, short], axis=0)
        mixed = jnp.dot(perm, total.astype(BF), preferred_element_type=F32)
        keep = (spot_row < 2 * rows_ref[v]) & (spot_col < 2 * cols_ref[v])
        out_ref[v, t] = jnp.where(keep, mixed, 0.0).astype(BF).reshape(2 * rows, 2 * cols, outs)

    for v in range(videos):
        products(v)
        for f in range(held):
            gate(v, f)
            if f >= 2:
                finish(v, f - 2)


def shards(tm, height, latents, conv_in, conv_out, shortcut, norm_gain, video_rows, video_cols):
    videos, frames, rows, cols, chans = latents.shape
    outs = conv_in.shape[-1]
    bottom_row = latents[:, :, rows - 1 :]
    top_row = latents[:, :, :1]
    up = [(h, h + 1) for h in range(height - 1)]
    down = [(h + 1, h) for h in range(height - 1)]
    prev = lax.ppermute(latents, "tm", [(t, t + 1) for t in range(tm - 1)])
    top = lax.ppermute(bottom_row, "height", up)
    bot = lax.ppermute(top_row, "height", down)
    both = ("tm", "height")
    ptop = lax.ppermute(
        bottom_row, both, [(t * height + i, (t + 1) * height + j) for t in range(tm - 1) for i, j in up]
    )
    pbot = lax.ppermute(
        top_row, both, [(t * height + i, (t + 1) * height + j) for t in range(tm - 1) for i, j in down]
    )
    position = lax.axis_index("height").astype(jnp.int32).reshape(1)
    wide = pl.cdiv(outs, 128) * 128
    smem = pl.BlockSpec(memory_space=pltpu.SMEM)
    vmem = pl.BlockSpec(memory_space=pltpu.VMEM)
    return pl.pallas_call(
        functools.partial(section, rows * height),
        out_shape=jax.ShapeDtypeStruct((videos, frames, 2 * rows, 2 * cols, outs), BF),
        in_specs=[smem] * 3 + [vmem] * 10,
        out_specs=vmem,
        scratch_shapes=[
            pltpu.VMEM((videos, 2 * frames, rows + 2, cols, chans), BF),
            pltpu.VMEM((videos, 3, 3, frames + 2, rows + 2, cols, wide), F32),
            pltpu.VMEM((videos, 4, frames + 2, 2 * rows + 2, cols, wide), BF),
            pltpu.VMEM((1, wide), F32),
        ],
        compiler_params=pltpu.CompilerParams(vmem_limit_bytes=48 << 20),
    )(
        video_rows,
        video_cols,
        position,
        latents,
        prev,
        top,
        bot,
        ptop,
        pbot,
        jnp.swapaxes(conv_in, 3, 4),
        conv_out,
        shortcut.T,
        norm_gain.reshape(1, outs),
    )


def solution(mesh):
    in_specs = (P(None, "tm", "height", None, None), P(), P(), P(), P(), P(), P())
    out_specs = P(None, "tm", "height", None, None)
    return jax.shard_map(
        functools.partial(shards, mesh.shape["tm"], mesh.shape["height"]),
        mesh=mesh,
        in_specs=in_specs,
        out_specs=out_specs,
        check_vma=False,
    )
```
